128 devices in a mesh: row: 8 (over y, core), col: 16 (over z, x).
Axes of the slice: x: 4, y: 4, z: 4, core: 2. Of those that a mesh axis runs over, the one named last changes fastest.
Arguments:
- density: bfloat16 [64, 64, 64, 1024], P('row', 'col'), may hold values from -6 to 6
- bra_factor: bfloat16 [128, 2, 256, 1024], P(('row', 'col')), may hold values from -0.375 to 0.375
- ket_factor: bfloat16 [128, 2, 256, 1024], P(('row', 'col')), may hold values from -0.1875 to 0.1875
- bra_blocks: int32 [128, 2, 2], P(('row', 'col')), may hold values from 0 to 63, as said below
- ket_blocks: int32 [128, 2, 2], P(('row', 'col')), may hold values from 0 to 63, as said below
- block_slot: int32 [64], replicated, may hold values from 0 to 63, as said below
- task_list: int32 [128, 4], P(('row', 'col')), may hold values from 0 to 3, each once within a row
- task_count: int32 [128], P(('row', 'col')), may hold values from 3 to 4, as said below
Outputs:
- exchange: bfloat16 [64, 64, 64, 1024], P('row', 'col')
The draws below stay inside these ranges and needn't reach their ends.
Inputs may be any that keep to these rules, and one draw needn't show every extreme that they name: `bra_blocks`: for each owner the 4 blocks of its bra pairs are stored in distinct device rows, where block x lies in device row block_slot[x] // 8. `ket_blocks`: for each owner the 4 blocks of its ket pairs are stored in distinct device columns, where block x lies in device column block_slot[x] // 4. `block_slot`: each number once. `task_list`: each row names every quartet index once. `task_count`: some owner has 4 live quartets.
All inputs are finite; a program needn't handle non-finite values.
Results may differ from the reference program's by a relative error of at most 0.0053.
Values may be sent and summed in bfloat16 or wider, within the bound.
No kernel may reach another device: no remote copies, remote signals or barrier semaphores. Data moves between devices by JAX's collectives and lax.ppermute only.
A program may use at most 192 MiB of HBM per device.

```python
import jax
import jax.numpy as jnp
from jax import lax

BLK_COL = 4
NB = 64
BLK_ROW = 8
P_SIZE = 64
BS = 32
RANK = 256
BRA = 2
KET = 2
QCAP = 4
N_ROW = 8
N_COL = 16
DEVICES = 128


def layout(key):
    slot = jax.random.permutation(jax.random.fold_in(key, 11), NB).astype(jnp.int32)
    inverse = jnp.argsort(slot).astype(jnp.int32)

    def one_owner(owner_key):
        keys = jax.random.split(owner_key, 4)
        rows = jax.random.permutation(keys[0], N_ROW).astype(jnp.int32)[:2 * BRA]
        row_store = rows * BLK_ROW + jax.random.randint(keys[1], (2 * BRA,), 0, BLK_ROW).astype(jnp.int32)
        columns = jax.random.permutation(keys[2], N_COL).astype(jnp.int32)[:2 * KET]
        column_store = columns * BLK_COL + jax.random.randint(keys[3], (2 * KET,), 0, BLK_COL).astype(jnp.int32)
        return (inverse[row_store].reshape(BRA, 2), inverse[column_store].reshape(KET, 2))
    owner_keys = jax.random.split(jax.random.fold_in(key, 12), DEVICES)
    bra_table, ket_table = jax.vmap(one_owner)(owner_keys)
    return (slot, bra_table, ket_table)


def draw_block_slot(key, part):
    return layout(key)[0]


def draw_bra_blocks(key, part):
    return layout(key)[1]


def draw_ket_blocks(key, part):
    return layout(key)[2]


def draw_task_count(key, part):
    base = jax.random.randint(jax.random.fold_in(key, 13), (DEVICES,), QCAP // 2 + 1, QCAP + 1).astype(jnp.int32)
    busiest = jax.random.randint(jax.random.fold_in(key, 14), (), 0, DEVICES)
    return base.at[busiest].set(QCAP).astype(jnp.int32)


def shard_levels(key, dims, pieces, low, top_value):
    loudness, own = 1.0, jax.random.fold_in(key, 6)
    for dim, blocks in pieces:
        heights = jnp.exp(jax.random.uniform(jax.random.fold_in(own, dim), (blocks,), jnp.float32, low / len(pieces), top_value / len(pieces)))
        loudness = loudness * jnp.repeat(heights, dims[dim] // blocks).reshape([-1 if axis == dim else 1 for axis in range(len(dims))])
    return loudness


def gaussian(key, extent, width, bound, pieces=(), held_as=jnp.bfloat16):
    drawn = jax.random.normal(key, extent, jnp.float32) * width
    if len(pieces) > 0:
        drawn = shard_levels(key, extent, pieces, -0.22, 0.18) * drawn
    return jnp.clip(drawn, min=-bound, max=bound).astype(held_as)


def setup_inputs(seed: int = 0) -> dict:
    key_of = jax.random.split(jax.random.key(seed), 9)
    density = gaussian(key_of[0], (NB, NB, P_SIZE, BS * BS), 1.0, 6.0, ((0, 8), (1, 16)))
    bra_factor = gaussian(key_of[1], (DEVICES, BRA, RANK, BS * BS), RANK ** -0.5, 0.375, ((0, 128),))
    ket_factor = gaussian(key_of[2], (DEVICES, KET, RANK, BS * BS), (BS * BS) ** -0.5, 0.1875, ((0, 128),))
    bra_blocks = draw_bra_blocks(jax.random.fold_in(key_of[8], 71), 0)
    ket_blocks = draw_ket_blocks(jax.random.fold_in(key_of[8], 71), 0)
    block_slot = draw_block_slot(jax.random.fold_in(key_of[8], 71), 0)
    task_list = jax.vmap(lambda own: jax.random.permutation(own, QCAP))(jax.random.split(key_of[6], DEVICES)).reshape((DEVICES, QCAP)).astype(jnp.int32)
    task_count = draw_task_count(jax.random.fold_in(key_of[8], 71), 0)
    return dict(density=density, bra_factor=bra_factor, ket_factor=ket_factor, bra_blocks=bra_blocks, ket_blocks=ket_blocks, block_slot=block_slot, task_list=task_list, task_count=task_count)


def reference(density, bra_factor, ket_factor, bra_blocks, ket_blocks, block_slot, task_list, task_count):
    area = BS * BS

    def quartet(exchange, item):
        owner = item // QCAP
        position = item % QCAP
        chosen = task_list[owner, position]
        bra_which = chosen // KET
        ket_which = chosen % KET
        first = block_slot[bra_blocks[owner, bra_which, 0]]
        second = block_slot[bra_blocks[owner, bra_which, 1]]
        third = block_slot[ket_blocks[owner, ket_which, 0]]
        fourth = block_slot[ket_blocks[owner, ket_which, 1]]

        def block(row, column):
            return density[row, column].astype(jnp.float32).reshape(P_SIZE, BS, BS)

        def work(unused):
            tile = lax.dot_general(bra_factor[owner, bra_which], ket_factor[owner, ket_which],
                                   (((0,), (0,)), ((), ())), preferred_element_type=jnp.float32)
            tile = lax.optimization_barrier(tile.astype(jnp.bfloat16)).astype(jnp.float32)
            tile = tile.reshape(BS, BS, BS, BS)
            update_bd = jnp.einsum('ijkl,pik->pjl', tile, block(first, third))
            update_bc = jnp.einsum('ijkl,pil->pjk', tile, block(first, fourth))
            update_ad = jnp.einsum('ijkl,pjk->pil', tile, block(second, third))
            update_ac = jnp.einsum('ijkl,pjl->pik', tile, block(second, fourth))
            stacked = jnp.stack([update_bd, update_bc, update_ad, update_ac]).reshape(4, P_SIZE, area)
            return lax.optimization_barrier(stacked.astype(jnp.bfloat16)).astype(jnp.float32)

        def skip(unused):
            return jnp.zeros((4, P_SIZE, area), jnp.float32)

        updates = lax.cond(position < task_count[owner], work, skip, 0)
        exchange = exchange.at[second, fourth].add(updates[0])
        exchange = exchange.at[second, third].add(updates[1])
        exchange = exchange.at[first, fourth].add(updates[2])
        exchange = exchange.at[first, third].add(updates[3])
        return exchange, None

    total = jnp.zeros((NB, NB, P_SIZE, area), jnp.float32)
    total, unused = lax.scan(quartet, total, jnp.arange(DEVICES * QCAP, dtype=jnp.int32))
    return total.astype(jnp.bfloat16)
```

```python
import functools

import jax
import jax.numpy as jnp
from jax import lax
from jax.experimental import pallas as pl
from jax.experimental.pallas import tpu as pltpu
from jax.sharding import PartitionSpec as P

SIDE = 32
AREA = SIDE * SIDE
LANES = 128
GROUP = LANES // SIDE
BF16 = jnp.bfloat16
F32 = jnp.float32
AXES = ("row", "col")


def swap_matrix():
    rows = lax.broadcasted_iota(jnp.int32, (AREA, AREA), 0)
    columns = lax.broadcasted_iota(jnp.int32, (AREA, AREA), 1)
    hit = columns == (rows % SIDE) * SIDE + rows // SIDE
    return jnp.where(hit, 1.0, 0.0).astype(BF16)


def mm(a, b, dims):
    return lax.dot_general(a, b, (dims, ((), ())), preferred_element_type=F32)


NN = ((1,), (0,))
NT = ((1,), (1,))


def tiles_kernel(live_ref, bra_ref, ket_ref, out_ref, swap_ref, bra_nat, bra_swap, g_ref):
    step = pl.program_id(0)

    @pl.when(step == 0)
    def _():
        swap_ref[...] = swap_matrix()

    @pl.when(step % 2 == 0)
    def _():
        bra = bra_ref[0]
        bra_nat[...] = bra.astype(F32).T.astype(BF16)
        bra_swap[...] = mm(swap_ref[...], bra, NT).astype(BF16)

    lane = lax.broadcasted_iota(jnp.int32, (SIDE, LANES), 1)
    low_half = lane < LANES // 2
    low_part = lane % (LANES // 2) < SIDE

    def build(source_ref, which):
        def chunk(high, carry):
            rows = source_ref[pl.ds(pl.multiple_of(high * LANES, LANES), LANES), :]
            g_ref[...] = mm(rows, ket_ref[0], NN)
            out_at = pl.ds(pl.multiple_of(high * LANES, LANES), LANES)
            for kh in range(AREA // LANES):
                at = pl.ds(kh * LANES, LANES)
                a = [g_ref[pl.ds(n * SIDE, SIDE), at] for n in range(GROUP)]
                b0 = jnp.where(low_half, a[0], pltpu.roll(a[2], 64, 1))
                b2 = jnp.where(low_half, pltpu.roll(a[0], 64, 1), a[2])
                b1 = jnp.where(low_half, a[1], pltpu.roll(a[3], 64, 1))
                b3 = jnp.where(low_half, pltpu.roll(a[1], 64, 1), a[3])
                c = [
                    jnp.where(low_part, b0, pltpu.roll(b1, 32, 1)),
                    jnp.where(low_part, pltpu.roll(b0, 96, 1), b1),
                    jnp.where(low_part, b2, pltpu.roll(b3, 32, 1)),
                    jnp.where(low_part, pltpu.roll(b2, 96, 1), b3),
                ]
                for n in range(GROUP):
                    row = (kh * GROUP + n) * SIDE
                    out_ref[0, which, pl.ds(row, SIDE), out_at] = c[n].astype(BF16)
            return carry

        lax.fori_loop(0, AREA // LANES, chunk, 0)

    @pl.when(live_ref[step] > 0)
    def _():
        build(bra_swap, 0)
        build(bra_nat, 1)


def tiles_call(live, bra, ket):
    rank = bra.shape[1]
    return pl.pallas_call(
        tiles_kernel,
        out_shape=jax.ShapeDtypeStruct((4, 2, AREA, AREA), BF16),
        grid=(4,),
        in_specs=[
            pl.BlockSpec(memory_space=pltpu.SMEM),
            pl.BlockSpec((1, rank, AREA), lambda t: (t // 2, 0, 0)),
            pl.BlockSpec((1, rank, AREA), lambda t: (t % 2, 0, 0)),
        ],
        out_specs=pl.BlockSpec((1, 2, AREA, AREA), lambda t: (t, 0, 0, 0)),
        scratch_shapes=[
            pltpu.VMEM((AREA, AREA), BF16),
            pltpu.VMEM((AREA, rank), BF16),
            pltpu.VMEM((AREA, rank), BF16),
            pltpu.VMEM((LANES, AREA), F32),
        ],
        compiler_params=pltpu.CompilerParams(vmem_limit_bytes=48 * 1024 * 1024),
        cost_estimate=pl.CostEstimate(flops=6_000_000_000, bytes_accessed=20_000_000, transcendentals=0),
    )(live, bra, ket)


def contract_kernel(live_ref, tile_ref, d_ref, out_ref, swap_ref):
    step = pl.program_id(0)
    dens = d_ref.shape[2]

    @pl.when(step == 0)
    def _():
        swap_ref[...] = swap_matrix()

    @pl.when(live_ref[step] > 0)
    def _():
        swap = swap_ref[...]
        d_ac = mm(d_ref[0, 0], swap, NN).astype(BF16)
        d_bc = mm(d_ref[1, 0], swap, NN).astype(BF16)
        t_one = tile_ref[0, 0]
        t_two = tile_ref[0, 1]
        out_ref[1, 1] = mm(d_ac, t_one, NN).astype(BF16)
        up_ac = mm(d_ref[1, 1], t_one, NT).astype(BF16)
        out_ref[0, 1] = mm(d_bc, t_two, NN).astype(BF16)
        up_bc = mm(d_ref[0, 1], t_two, NT).astype(BF16)
        out_ref[0, 0] = mm(up_ac, swap, NN).astype(BF16)
        out_ref[1, 0] = mm(up_bc, swap, NN).astype(BF16)

    @pl.when(live_ref[step] == 0)
    def _():
        out_ref[...] = jnp.zeros_like(out_ref)


def contract_call(live, tiles, blocks):
    dens = blocks.shape[2]
    return pl.pallas_call(
        contract_kernel,
        out_shape=jax.ShapeDtypeStruct(blocks.shape, BF16),
        grid=(4,),
        in_specs=[
            pl.BlockSpec(memory_space=pltpu.SMEM),
            pl.BlockSpec((1, 2, AREA, AREA), lambda t: (t, 0, 0, 0)),
            pl.BlockSpec((2, 2, dens, AREA), lambda t: (t // 2, t % 2, 0, 0)),
        ],
        out_specs=pl.BlockSpec((2, 2, dens, AREA), lambda t: (t // 2, t % 2, 0, 0)),
        scratch_shapes=[pltpu.VMEM((AREA, AREA), BF16)],
        compiler_params=pltpu.CompilerParams(vmem_limit_bytes=48 * 1024 * 1024),
        cost_estimate=pl.CostEstimate(flops=6_000_000_000, bytes_accessed=20_000_000, transcendentals=0),
    )(live, tiles, blocks)


def split_parts(blocks):
    n, dens, area = blocks.shape
    x = blocks.reshape(n, dens // 8, 2, 4, area // LANES, LANES)
    x = x.transpose(1, 4, 2, 0, 3, 5)
    return x.reshape(dens * area // 512, n, 4, LANES)


def join_parts(parts, dens, area):
    _, n, _, _ = parts.shape
    x = parts.reshape(dens // 8, area // LANES, 2, n, 4, LANES)
    x = x.transpose(3, 0, 2, 4, 1, 5)
    return x.reshape(n, dens, area)


def exchange_all(x):
    return lax.all_to_all(x, AXES, split_axis=0, concat_axis=0, tiled=True)


def shards(density, bra_factor, ket_factor, bra_blocks, ket_blocks, block_slot, task_list, task_count):
    n_col = lax.axis_size("col")
    devices = lax.axis_size("row") * n_col
    blk_row, blk_col, dens, area = density.shape
    local = blk_row * blk_col

    names = jnp.concatenate([bra_blocks[0].reshape(4), ket_blocks[0].reshape(4)])
    hits = names[:, None] == jnp.arange(block_slot.shape[0], dtype=jnp.int32)
    slots = jnp.sum(jnp.where(hits, block_slot[None, :], 0), axis=-1)
    listed = jnp.arange(4, dtype=jnp.int32) < task_count[0]
    live = jnp.any(
        (task_list[0][None, :] == jnp.arange(4, dtype=jnp.int32)[:, None]) & listed[None, :], axis=1
    ).astype(jnp.int32)

    row = jnp.zeros((4, LANES), BF16).at[0, :8].set(slots.astype(BF16))
    row = jnp.broadcast_to(row[None, None], (devices, 1, 4, LANES))
    outgoing = jnp.concatenate([split_parts(density.reshape(local, dens, area)), row], axis=1)
    arrived = exchange_all(outgoing)
    table = arrived[:, local, 0, :8].astype(F32).astype(jnp.int32)
    xs, ys = table[:, :4, None], table[:, None, 4:]
    place = ((xs // blk_row) * n_col + ys // blk_col, (xs % blk_row) * blk_col + ys % blk_col)
    fetch_at = (place[0] * (local + 1) + place[1]).reshape(devices * 16)
    store_at = (place[0] * local + place[1]).reshape(devices * 16)
    picked = jnp.take(arrived.reshape(devices * (local + 1), 4, LANES), fetch_at, axis=0)
    fetched = exchange_all(picked.reshape(devices, 16, 4, LANES))
    corners = join_parts(fetched, dens, area).reshape(4, 4, dens, area)

    tiles = tiles_call(live, bra_factor[0], ket_factor[0])
    updates = contract_call(live, tiles, corners)

    returned = exchange_all(split_parts(updates.reshape(16, dens, area)))
    hot = (jnp.arange(devices * local, dtype=jnp.int32)[:, None] == store_at[None, :]).astype(BF16)
    total = lax.dot_general(
        hot, returned.reshape(devices * 16, 512), (((1,), (0,)), ((), ())), preferred_element_type=F32
    )
    total = total.astype(BF16).reshape(devices, local, 4, LANES)
    final = join_parts(exchange_all(total), dens, area)
    return final.reshape(blk_row, blk_col, dens, area)


def solution(mesh):
    in_specs = (
        P("row", "col", None, None),
        P(AXES, None, None, None),
        P(AXES, None, None, None),
        P(AXES, None, None),
        P(AXES, None, None),
        P(),
        P(AXES, None),
        P(AXES),
    )
    out_specs = P("row", "col", None, None)
    return jax.shard_map(shards, mesh=mesh, in_specs=in_specs, out_specs=out_specs, check_vma=False)
```

```python
import functools

import jax
import jax.numpy as jnp
from jax import lax
from jax.experimental import pallas as pl
from jax.experimental.pallas import tpu as pltpu
from jax.sharding import PartitionSpec as P

SIDE = 32
AREA = SIDE * SIDE
LANES = 128
GROUP = LANES // SIDE
BF16 = jnp.bfloat16
F32 = jnp.float32
AXES = ("row", "col")
CAP = 20
PIECE = 256


def swap_matrix():
    rows = lax.broadcasted_iota(jnp.int32, (AREA, AREA), 0)
    columns = lax.broadcasted_iota(jnp.int32, (AREA, AREA), 1)
    hit = columns == (rows % SIDE) * SIDE + rows // SIDE
    return jnp.where(hit, 1.0, 0.0).astype(BF16)


def mm(a, b, dims):
    return lax.dot_general(a, b, (dims, ((), ())), preferred_element_type=F32)


NN = ((1,), (0,))
NT = ((1,), (1,))


def tiles_kernel(first, live_ref, after_ref, bra_ref, ket_ref, old_ref, out_ref, token_ref, swap_ref, bra_nat, bra_swap, g_ref, t_ref):
    step = pl.program_id(0)
    token_ref[0] = 0

    @pl.when(step == 0)
    def _():
        swap_ref[...] = swap_matrix()

    @pl.when((step == 0) | ((first + step) % 2 == 0))
    def _():
        bra = bra_ref[0]
        bra_nat[...] = bra.astype(F32).T.astype(BF16)
        bra_swap[...] = mm(swap_ref[...], bra, NT).astype(BF16)

    lane = lax.broadcasted_iota(jnp.int32, (SIDE, LANES), 1)
    low_half = lane < LANES // 2
    low_part = lane % (LANES // 2) < SIDE

    def build(source_ref, which):
        def chunk(high, carry):
            rows = source_ref[pl.ds(pl.multiple_of(high * LANES, LANES), LANES), :]
            g_ref[...] = mm(rows, ket_ref[0], NN)
            out_at = pl.ds(pl.multiple_of(high * LANES, LANES), LANES)
            for kh in range(AREA // LANES):
                at = pl.ds(kh * LANES, LANES)
                a = [g_ref[pl.ds(n * SIDE, SIDE), at] for n in range(GROUP)]
                b0 = jnp.where(low_half, a[0], pltpu.roll(a[2], 64, 1))
                b2 = jnp.where(low_half, pltpu.roll(a[0], 64, 1), a[2])
                b1 = jnp.where(low_half, a[1], pltpu.roll(a[3], 64, 1))
                b3 = jnp.where(low_half, pltpu.roll(a[1], 64, 1), a[3])
                c = [
                    jnp.where(low_part, b0, pltpu.roll(b1, 32, 1)),
                    jnp.where(low_part, pltpu.roll(b0, 96, 1), b1),
                    jnp.where(low_part, b2, pltpu.roll(b3, 32, 1)),
                    jnp.where(low_part, pltpu.roll(b2, 96, 1), b3),
                ]
                for n in range(GROUP):
                    row = (kh * GROUP + n) * SIDE
                    t_ref[pl.ds(row, SIDE), out_at] = c[n].astype(BF16)
            return carry

        lax.fori_loop(0, AREA // LANES, chunk, 0)

        def order(high, carry):
            at = pl.ds(pl.multiple_of(high * 256, 256), 256)
            for low in range(AREA // 256):
                to = pl.ds(low * 256, 256)
                out_ref[0, which, at, to] = mm(swap_ref[at, :], t_ref[:, to], NN).astype(BF16)
            return carry

        lax.fori_loop(0, AREA // 256, order, 0)

    @pl.when(live_ref[first + step] > 0)
    def _():
        build(bra_swap, 0)
        build(bra_nat, 1)


def tiles_call(first, count, live, after, bra, ket, old):
    rank = bra.shape[1]
    smem = pl.BlockSpec(memory_space=pltpu.SMEM)
    return pl.pallas_call(
        functools.partial(tiles_kernel, first),
        out_shape=(pltpu.HBM((4, 2, AREA, AREA), BF16), jax.ShapeDtypeStruct((1,), jnp.int32)),
        grid=(count,),
        in_specs=[
            smem,
            smem,
            pl.BlockSpec((1, rank, AREA), lambda t: ((first + t) // 2, 0, 0)),
            pl.BlockSpec((1, rank, AREA), lambda t: ((first + t) % 2, 0, 0)),
            pl.BlockSpec(memory_space=pl.ANY),
        ],
        out_specs=(pl.BlockSpec((1, 2, AREA, AREA), lambda t: (first + t, 0, 0, 0)), smem),
        scratch_shapes=[
            pltpu.VMEM((AREA, AREA), BF16),
            pltpu.VMEM((AREA, rank), BF16),
            pltpu.VMEM((AREA, rank), BF16),
            pltpu.VMEM((LANES, AREA), F32),
            pltpu.VMEM((AREA, AREA), BF16),
        ],
        input_output_aliases={4: 0} if first else {},
        compiler_params=pltpu.CompilerParams(vmem_limit_bytes=20 * 1024 * 1024),
        cost_estimate=pl.CostEstimate(flops=6_000_000_000 * count, bytes_accessed=6_000_000, transcendentals=0),
    )(live, after, bra, ket, old)


def contract_kernel(live_ref, tile_ref, in_ref, out_ref, t_ref, d_ref, u_ref, t_sems, in_sems, out_sems):
    step, which = pl.program_id(0), pl.program_id(1)
    turn = step * 2 + which
    high, wide = in_ref.shape[:2]

    def spots_of(step, which):
        base = (step // 2) * 8 + (step % 2) * 2
        return base + which, base + 5 - which

    def fetch(spot, half):
        to = d_ref.at[spot, :, :, pl.ds(half * 4, 4)]
        return pltpu.make_async_copy(in_ref.at[:, :, half, spot], to, in_sems.at[spot, half])

    def send(step, which, n, half):
        to = out_ref.at[:, :, half, spots_of(step, which)[n]]
        return pltpu.make_async_copy(u_ref.at[which, n, :, :, pl.ds(half * 4, 4)], to, out_sems.at[which, n, half])

    def bring(step, which):
        return pltpu.make_async_copy(tile_ref.at[step, which], t_ref.at[step, which], t_sems.at[step, which])

    pieces = [(n, half) for n in range(2) for half in range(2)]

    @pl.when(turn == 0)
    def _():
        for t in range(4):
            for w in range(2):
                for n, half in pieces:
                    fetch(spots_of(t, w)[n], half).start()

            @pl.when(live_ref[t] > 0)
            def _():
                for w in range(2):
                    bring(t, w).start()

    @pl.when(step > 0)
    def _():
        for n, half in pieces:
            send(step - 1, which, n, half).wait()

    spots = spots_of(step, which)
    for n, half in pieces:
        fetch(spots[n], half).wait()

    @pl.when(live_ref[step] > 0)
    def _():
        bring(step, which).wait()
        ahead = jnp.where(which == 0, spots[0], spots[1])
        behind = jnp.where(which == 0, spots[1], spots[0])

        def side(spot):
            flat = [d_ref[spot, :, low].reshape(high * 8, LANES) for low in range(wide)]
            return jnp.concatenate(flat, axis=1)

        def keep(n, at, value):
            for low in range(PIECE // LANES):
                part = value[:, low * LANES : (low + 1) * LANES].astype(BF16)
                u_ref[which, n, :, at // LANES + low] = part.reshape(high, 8, LANES)

        upper, lower = side(ahead), side(behind)
        for n in range(0, AREA, PIECE):
            keep(1 - which, n, mm(upper, t_ref[step, which, :, pl.ds(n, PIECE)], NN))
            keep(which, n, mm(lower, t_ref[step, which, pl.ds(n, PIECE), :], NT))

    @pl.when(live_ref[step] == 0)
    def _():
        u_ref[which] = jnp.zeros(u_ref.shape[1:], BF16)

    for n, half in pieces:
        send(step, which, n, half).start()

    @pl.when(turn == 7)
    def _():
        for w in range(2):
            for n, half in pieces:
                send(3, w, n, half).wait()


def contract_call(live, tiles, fetched, dens):
    parts, corners, _, _ = fetched.shape
    shape = (dens // 8, AREA // LANES, 2, corners, 4, LANES)
    updates = pl.pallas_call(
        contract_kernel,
        out_shape=pltpu.HBM(shape, BF16),
        grid=(4, 2),
        in_specs=[
            pl.BlockSpec(memory_space=pltpu.SMEM),
            pl.BlockSpec(memory_space=pl.ANY),
            pl.BlockSpec(memory_space=pl.ANY),
        ],
        out_specs=pl.BlockSpec(memory_space=pl.ANY),
        scratch_shapes=[
            pltpu.VMEM(tiles.shape, BF16),
            pltpu.VMEM((corners, dens // 8, AREA // LANES, 8, LANES), BF16),
            pltpu.VMEM((2, 2, dens // 8, AREA // LANES, 8, LANES), BF16),
            pltpu.SemaphoreType.DMA((4, 2)),
            pltpu.SemaphoreType.DMA((corners, 2)),
            pltpu.SemaphoreType.DMA((2, 2, 2)),
        ],
        compiler_params=pltpu.CompilerParams(vmem_limit_bytes=48 * 1024 * 1024),
        cost_estimate=pl.CostEstimate(flops=6_000_000_000, bytes_accessed=20_000_000, transcendentals=0),
    )(live, tiles, fetched.reshape(shape))
    return updates.reshape(fetched.shape)


def split_kernel(bra_ref, ket_ref, slot_ref, list_ref, count_ref, in_ref, out_ref, live_ref, buf_ref, in_sems, out_sems):
    count, dens, area = in_ref.shape
    each = 2 * area // LANES
    groups = dens // 8
    for g in range(groups):
        for part in range(each):
            rows, low = pl.ds(g * 8 + part % 2 * 4, 4), part // 2
            pltpu.make_async_copy(
                in_ref.at[:, rows, pl.ds(low * LANES, LANES)],
                buf_ref.at[g * each + part, pl.ds(0, count)],
                in_sems.at[g, part],
            ).start()
    slots = [slot_ref[bra_ref[0, n // 2, n % 2]] for n in range(4)]
    slots += [slot_ref[ket_ref[0, n // 2, n % 2]] for n in range(4)]
    live = []
    for task in range(4):
        hit = 0
        for n in range(4):
            hit = hit + jnp.where((list_ref[0, n] == task) & (n < count_ref[0]), 1, 0)
        live.append(hit)
        live_ref[task] = hit
    lane = lax.broadcasted_iota(jnp.int32, (4, LANES), 1)
    head = jnp.zeros((4, LANES), jnp.int32)
    for n, value in enumerate(slots + live):
        head = jnp.where(lane == n, value, head)
    head = head.astype(F32).astype(BF16)
    for part in range(groups * each):
        buf_ref[part, count] = head
    outs = []
    for g in range(groups):
        for part in range(each):
            rows, low = pl.ds(g * 8 + part % 2 * 4, 4), part // 2
            pltpu.make_async_copy(
                in_ref.at[:, rows, pl.ds(low * LANES, LANES)],
                buf_ref.at[g * each + part, pl.ds(0, count)],
                in_sems.at[g, part],
            ).wait()
        at = pl.ds(g * each, each)
        outs.append(pltpu.make_async_copy(buf_ref.at[at], out_ref.at[at], out_sems.at[g]))
        outs[g].start()
    for g in range(groups):
        outs[g].wait()


def split_call(bra, ket, slot, tasks, counts, blocks):
    count, dens, area = blocks.shape
    each = 2 * area // LANES
    shape = (dens // 8 * each, count + 1, 4, LANES)
    smem = pl.BlockSpec(memory_space=pltpu.SMEM)
    hbm = pl.BlockSpec(memory_space=pl.ANY)
    return pl.pallas_call(
        split_kernel,
        out_shape=(pltpu.HBM(shape, BF16), jax.ShapeDtypeStruct((4,), jnp.int32)),
        in_specs=[smem] * 5 + [hbm],
        out_specs=(hbm, smem),
        scratch_shapes=[
            pltpu.VMEM(shape, BF16),
            pltpu.SemaphoreType.DMA((dens // 8, each)),
            pltpu.SemaphoreType.DMA((dens // 8,)),
        ],
        compiler_params=pltpu.CompilerParams(vmem_limit_bytes=60 * 1024 * 1024),
    )(bra, ket, slot, tasks, counts, blocks)


def join_kernel(most_ref, slot_ref, in_ref, more_ref, out_ref, zero_ref, sems):
    count = out_ref.shape[0]
    wide, cap = in_ref.shape[1], in_ref.shape[3]
    zero_ref[...] = jnp.zeros(zero_ref.shape, BF16)

    def fill(block, ref, slot):
        for low in range(wide):
            for half in range(2):
                to = out_ref.at[block, :, pl.ds(half * 4, 4), pl.ds(low * LANES, LANES)]
                pltpu.make_async_copy(ref.at[:, low, half, slot], to, sems.at[block]).start()

    def one(block, carry):
        slot = slot_ref[block]

        @pl.when(slot < 0)
        def _():
            pltpu.make_async_copy(zero_ref, out_ref.at[block], sems.at[block]).start()

        @pl.when((slot >= 0) & (slot < cap))
        def _():
            fill(block, in_ref, slot)

        @pl.when(slot >= cap)
        def _():
            fill(block, more_ref, slot - cap)

        return carry

    lax.fori_loop(0, count, one, 0)

    def done(block, carry):
        pltpu.make_async_copy(zero_ref, out_ref.at[block], sems.at[block]).wait()
        return carry

    lax.fori_loop(0, count, done, 0)


def join_call(most, slots, parts, more, count, dens, area):
    smem = pl.BlockSpec(memory_space=pltpu.SMEM)
    tall, wide = dens // 8, area // LANES

    def view(x):
        return x.reshape(tall, wide, 2, x.shape[1], 4, LANES)

    blocks = pl.pallas_call(
        join_kernel,
        out_shape=pltpu.HBM((count, tall, 8, area), BF16),
        in_specs=[smem, smem, pl.BlockSpec(memory_space=pltpu.VMEM), pl.BlockSpec(memory_space=pl.ANY)],
        out_specs=pl.BlockSpec(memory_space=pl.ANY),
        scratch_shapes=[pltpu.VMEM((tall, 8, area), BF16), pltpu.SemaphoreType.DMA((count,))],
        compiler_params=pltpu.CompilerParams(vmem_limit_bytes=32 * 1024 * 1024),
    )(most, slots, view(parts), view(more))
    return blocks.reshape(count, dens, area)


def gather_kernel(token_ref, in_ref, out_ref, table_ref, after_ref, rows_ref, head_ref, at_ref, spot_ref, sems):
    after_ref[0] = token_ref[0]
    owners, stride = in_ref.shape[0], in_ref.shape[1]
    step = pl.program_id(0)
    near = out_ref.shape[0]

    @pl.when(step == 0)
    def _():
        heads = pltpu.make_async_copy(in_ref.at[:, stride - 1], head_ref, sems.at[0])
        heads.start()
        rest = pltpu.make_async_copy(in_ref, rows_ref, sems.at[1])
        rest.start()
        heads.wait()

        def pull(owner, carry):
            head = head_ref[owner].astype(F32)[0:1]
            table_ref[pl.ds(owner, 1), :] = head.astype(jnp.int32)
            return carry

        lax.fori_loop(0, owners, pull, 0, unroll=8)
        table = table_ref[...]
        lane = lax.broadcasted_iota(jnp.int32, table.shape, 1)
        down = (table >> 3) * 16
        across = table >> 2
        inside = jnp.where(lane < 4, (table & 7) * 4, table & 3)
        at_ref[...] = jnp.where(lane < 4, down, across) * stride + inside
        copy = pltpu.make_async_copy(at_ref, spot_ref, sems.at[2])
        copy.start()
        copy.wait()
        rest.wait()

    flat = rows_ref.reshape(owners * stride, 4, LANES)

    def one(n, carry):
        owner = step * near + n
        downs = [spot_ref[owner, n] for n in range(4)]
        acrosses = [spot_ref[owner, 4 + n] for n in range(4)]
        for corner in range(16):
            out_ref[n, corner] = flat[downs[corner // 4] + acrosses[corner % 4]]
        return carry

    lax.fori_loop(0, near, one, 0, unroll=2)


def gather_call(token, rows):
    smem = pl.BlockSpec(memory_space=pltpu.SMEM)
    owners = rows.shape[0]
    near = owners // 8
    return pl.pallas_call(
        gather_kernel,
        out_shape=(
            pltpu.HBM((owners, 16, 4, LANES), BF16),
            pltpu.HBM((owners, LANES), jnp.int32),
            jax.ShapeDtypeStruct((1,), jnp.int32),
        ),
        grid=(8,),
        in_specs=[smem, pl.BlockSpec(memory_space=pl.ANY)],
        out_specs=(
            pl.BlockSpec((near, 16, 4, LANES), lambda g: (g, 0, 0, 0)),
            pl.BlockSpec((owners, LANES), lambda g: (0, 0)),
            smem,
        ),
        scratch_shapes=[
            pltpu.VMEM(rows.shape, BF16),
            pltpu.VMEM((owners, 4, LANES), BF16),
            pltpu.VMEM((owners, LANES), jnp.int32),
            pltpu.SMEM((owners, LANES), jnp.int32),
            pltpu.SemaphoreType.DMA((3,)),
        ],
        compiler_params=pltpu.CompilerParams(vmem_limit_bytes=60 * 1024 * 1024),
    )(token, rows)


def plan_kernel(table_ref, at_ref, ranks_ref):
    table = table_ref[...]
    owners = table.shape[0]
    size = ranks_ref.shape[0]
    ids = lax.broadcasted_iota(jnp.int32, (owners, size), 1)
    hot = [(table[:, n : n + 1] == ids).astype(F32) for n in range(8)]
    live = [table[:, n : n + 1].astype(F32) for n in range(8, 12)]
    xs, ys = hot[:4], hot[4:]
    both = [ys[0] + ys[1], ys[2] + ys[3]]
    count = 0.0
    for pair in range(2):
        across = live[2 * pair] * both[0] + live[2 * pair + 1] * both[1]
        count = count + mm(xs[2 * pair] + xs[2 * pair + 1], across, ((0,), (0,)))
    used = (count > 0.5).astype(F32)
    a = lax.broadcasted_iota(jnp.int32, (size, size), 0)
    b = lax.broadcasted_iota(jnp.int32, (size, size), 1)
    above = ((a // 8 == b // 8) & (b < a)).astype(F32)
    beside = (a // 4 == b // 4).astype(F32)
    before = ((a // 4 == b // 4) & (a < b)).astype(F32)
    rank = mm(mm(above, used, NN), beside, NN) + mm(used, before, NN)
    ranks_ref[...] = jnp.where(used > 0.5, rank, -1.0).astype(jnp.int32)
    for i in range(4):
        mine = mm(xs[i], rank, NN)
        for j in range(4):
            n = i * 4 + j
            found = jnp.sum(mine * ys[j], axis=1, keepdims=True)
            dev = table[:, i : i + 1] // 8 * 16 + table[:, 4 + j : 5 + j] // 4
            at_ref[:, n : n + 1] = dev * 32 + found.astype(jnp.int32)


def plan_call(table, size):
    owners = table.shape[0]
    return pl.pallas_call(
        plan_kernel,
        out_shape=(
            pltpu.HBM((owners, 16), jnp.int32),
            jax.ShapeDtypeStruct((size, size), jnp.int32),
        ),
    )(table)


def scatter_kernel(most_ref, at_ref, in_ref, out_ref, more_ref, sum_ref, spot_ref, sem):
    near, cap = out_ref.shape[0], out_ref.shape[1]
    room = cap + more_ref.shape[1]
    devices = sum_ref.shape[0] // room
    crowded = most_ref[0] > cap
    step = pl.program_id(0)

    @pl.when(step == 0)
    def _():
        copy = pltpu.make_async_copy(at_ref, spot_ref, sem)
        copy.start()

        def clear(dev, carry):
            sum_ref[pl.ds(dev * room, cap)] = jnp.zeros((cap, 4, LANES), F32)
            return carry

        lax.fori_loop(0, devices, clear, 0, unroll=4)

        @pl.when(crowded)
        def _():
            def clear_more(dev, carry):
                sum_ref[pl.ds(dev * room + cap, room - cap)] = jnp.zeros((room - cap, 4, LANES), F32)
                return carry
            lax.fori_loop(0, devices, clear_more, 0)

        copy.wait()

        def one(owner, carry):
            spots = [spot_ref[owner, n] for n in range(16)]
            sums = [sum_ref[spots[n]] + in_ref[owner, n].astype(F32) for n in range(16)]
            for n in range(16):
                sum_ref[spots[n]] = sums[n]
            return carry

        lax.fori_loop(0, in_ref.shape[0], one, 0, unroll=4)

    def finish(n, carry):
        out_ref[n] = sum_ref[pl.ds((step * near + n) * room, cap)].astype(BF16)
        return carry

    lax.fori_loop(0, near, finish, 0, unroll=4)

    @pl.when(crowded)
    def _():
        def finish_more(n, carry):
            more_ref[n] = sum_ref[pl.ds((step * near + n) * room + cap, room - cap)].astype(BF16)
            return carry
        lax.fori_loop(0, near, finish_more, 0)


def scatter_call(most, at, updates, devices, cap, room):
    smem = pl.BlockSpec(memory_space=pltpu.SMEM)
    near = devices // 8
    return pl.pallas_call(
        scatter_kernel,
        out_shape=(
            pltpu.HBM((devices, cap, 4, LANES), BF16),
            pltpu.HBM((devices, room - cap, 4, LANES), BF16),
        ),
        grid=(8,),
        in_specs=[smem, pl.BlockSpec(memory_space=pltpu.HBM), pl.BlockSpec(memory_space=pltpu.VMEM)],
        out_specs=(
            pl.BlockSpec((near, cap, 4, LANES), lambda g: (g, 0, 0, 0)),
            pl.BlockSpec((near, room - cap, 4, LANES), lambda g: (g, 0, 0, 0)),
        ),
        scratch_shapes=[
            pltpu.VMEM((devices * room, 4, LANES), F32),
            pltpu.SMEM(at.shape, jnp.int32),
            pltpu.SemaphoreType.DMA,
        ],
        compiler_params=pltpu.CompilerParams(vmem_limit_bytes=40 * 1024 * 1024),
    )(most, at, updates)


def exchange_all(x):
    return lax.all_to_all(x, AXES, split_axis=0, concat_axis=0, tiled=True)


def shards(density, bra_factor, ket_factor, bra_blocks, ket_blocks, block_slot, task_list, task_count):
    n_col = lax.axis_size("col")
    devices = lax.axis_size("row") * n_col
    blk_row, blk_col, dens, area = density.shape
    local = blk_row * blk_col

    outgoing, live = split_call(
        bra_blocks, ket_blocks, block_slot, task_list, task_count, density.reshape(local, dens, area)
    )
    arrived = exchange_all(outgoing)
    tiles, token = tiles_call(0, 3, live, live, bra_factor[0], ket_factor[0], live)
    picked, table, token = gather_call(token, arrived)
    fetched = exchange_all(picked)

    tiles, _ = tiles_call(3, 1, live, token, bra_factor[0], ket_factor[0], tiles)
    at, ranks = plan_call(table, block_slot.shape[0])
    most = (jnp.max(ranks) + 1).reshape(1)
    corner = (lax.axis_index("row") * blk_row, lax.axis_index("col") * blk_col)
    mine = lax.dynamic_slice(ranks, corner, (blk_row, blk_col)).reshape(local)
    updates = contract_call(live, tiles, fetched, dens)

    returned = exchange_all(updates)
    total, more = scatter_call(most, at, returned, devices, CAP, local)
    parts = exchange_all(total)
    more = lax.cond(most[0] > CAP, exchange_all, lambda x: x, more)
    final = join_call(most, mine, parts, more, local, dens, area)
    return final.reshape(blk_row, blk_col, dens, area)


def solution(mesh):
    in_specs = (
        P("row", "col", None, None),
        P(AXES, None, None, None),
        P(AXES, None, None, None),
        P(AXES, None, None),
        P(AXES, None, None),
        P(),
        P(AXES, None),
        P(AXES),
    )
    out_specs = P("row", "col", None, None)
    return jax.shard_map(shards, mesh=mesh, in_specs=in_specs, out_specs=out_specs, check_vma=False)
```

```python
import functools

import jax
import jax.numpy as jnp
from jax import lax
from jax.experimental import pallas as pl
from jax.experimental.pallas import tpu as pltpu
from jax.sharding import PartitionSpec as P

SIDE = 32
AREA = SIDE * SIDE
LANES = 128
GROUP = LANES // SIDE
BF16 = jnp.bfloat16
F32 = jnp.float32
AXES = ("row", "col")
CAP = 20
PIECE = 256


def swap_matrix():
    rows = lax.broadcasted_iota(jnp.int32, (AREA, AREA), 0)
    columns = lax.broadcasted_iota(jnp.int32, (AREA, AREA), 1)
    hit = columns == (rows % SIDE) * SIDE + rows // SIDE
    return jnp.where(hit, 1.0, 0.0).astype(BF16)


def mm(a, b, dims):
    return lax.dot_general(a, b, (dims, ((), ())), preferred_element_type=F32)


NN = ((1,), (0,))
NT = ((1,), (1,))


def tiles_kernel(first, live_ref, after_ref, bra_ref, ket_ref, old_ref, out_ref, token_ref, swap_ref, bra_nat, bra_swap, g_ref, t_ref):
    step = pl.program_id(0)
    token_ref[0] = 0

    @pl.when(step == 0)
    def _():
        swap_ref[...] = swap_matrix()

    @pl.when((step == 0) | ((first + step) % 2 == 0))
    def _():
        bra = bra_ref[0]
        bra_nat[...] = bra.astype(F32).T.astype(BF16)
        bra_swap[...] = mm(swap_ref[...], bra, NT).astype(BF16)

    lane = lax.broadcasted_iota(jnp.int32, (SIDE, LANES), 1)
    low_half = lane < LANES // 2
    low_part = lane % (LANES // 2) < SIDE

    def build(source_ref, which):
        def chunk(high, carry):
            rows = source_ref[pl.ds(pl.multiple_of(high * LANES, LANES), LANES), :]
            g_ref[...] = mm(rows, ket_ref[0], NN)
            out_at = pl.ds(pl.multiple_of(high * LANES, LANES), LANES)
            for kh in range(AREA // LANES):
                at = pl.ds(kh * LANES, LANES)
                a = [g_ref[pl.ds(n * SIDE, SIDE), at] for n in range(GROUP)]
                b0 = jnp.where(low_half, a[0], pltpu.roll(a[2], 64, 1))
                b2 = jnp.where(low_half, pltpu.roll(a[0], 64, 1), a[2])
                b1 = jnp.where(low_half, a[1], pltpu.roll(a[3], 64, 1))
                b3 = jnp.where(low_half, pltpu.roll(a[1], 64, 1), a[3])
                c = [
                    jnp.where(low_part, b0, pltpu.roll(b1, 32, 1)),
                    jnp.where(low_part, pltpu.roll(b0, 96, 1), b1),
                    jnp.where(low_part, b2, pltpu.roll(b3, 32, 1)),
                    jnp.where(low_part, pltpu.roll(b2, 96, 1), b3),
                ]
                for n in range(GROUP):
                    row = (kh * GROUP + n) * SIDE
                    t_ref[pl.ds(row, SIDE), out_at] = c[n].astype(BF16)
            return carry

        lax.fori_loop(0, AREA // LANES, chunk, 0)

        def order(high, carry):
            at = pl.ds(pl.multiple_of(high * 256, 256), 256)
            for low in range(AREA // 256):
                to = pl.ds(low * 256, 256)
                out_ref[0, which, at, to] = mm(swap_ref[at, :], t_ref[:, to], NN).astype(BF16)
            return carry

        lax.fori_loop(0, AREA // 256, order, 0)

    @pl.when(live_ref[first + step] > 0)
    def _():
        build(bra_swap, 0)
        build(bra_nat, 1)


def tiles_call(first, count, live, after, bra, ket, old):
    rank = bra.shape[1]
    smem = pl.BlockSpec(memory_space=pltpu.SMEM)
    return pl.pallas_call(
        functools.partial(tiles_kernel, first),
        out_shape=(pltpu.HBM((4, 2, AREA, AREA), BF16), jax.ShapeDtypeStruct((1,), jnp.int32)),
        grid=(count,),
        in_specs=[
            smem,
            smem,
            pl.BlockSpec((1, rank, AREA), lambda t: ((first + t) // 2, 0, 0)),
            pl.BlockSpec((1, rank, AREA), lambda t: ((first + t) % 2, 0, 0)),
            pl.BlockSpec(memory_space=pl.ANY),
        ],
        out_specs=(pl.BlockSpec((1, 2, AREA, AREA), lambda t: (first + t, 0, 0, 0)), smem),
        scratch_shapes=[
            pltpu.VMEM((AREA, AREA), BF16),
            pltpu.VMEM((AREA, rank), BF16),
            pltpu.VMEM((AREA, rank), BF16),
            pltpu.VMEM((LANES, AREA), F32),
            pltpu.VMEM((AREA, AREA), BF16),
        ],
        input_output_aliases={4: 0} if first else {},
        compiler_params=pltpu.CompilerParams(vmem_limit_bytes=20 * 1024 * 1024),
        cost_estimate=pl.CostEstimate(flops=6_000_000_000 * count, bytes_accessed=6_000_000, transcendentals=0),
    )(live, after, bra, ket, old)


def contract_kernel(live_ref, tile_ref, in_ref, out_ref, t_ref, d_ref, u_ref, t_sems, in_sems, out_sems):
    high, wide = in_ref.shape[:2]

    def spots_of(step, which):
        base = (step // 2) * 8 + (step % 2) * 2
        return base + which, base + 5 - which

    def fetch(spot, half):
        to = d_ref.at[spot, :, :, pl.ds(half * 4, 4)]
        return pltpu.make_async_copy(in_ref.at[:, :, half, spot], to, in_sems.at[spot, half])

    def send(step, which, n, half):
        to = out_ref.at[:, :, half, spots_of(step, which)[n]]
        return pltpu.make_async_copy(u_ref.at[which, n, :, :, pl.ds(half * 4, 4)], to, out_sems.at[which, n, half])

    def bring(step, which):
        return pltpu.make_async_copy(tile_ref.at[step, which], t_ref.at[step, which], t_sems.at[step, which])

    pieces = [(n, half) for n in range(2) for half in range(2)]

    def one(turn, carry):
        step, which = turn >> 1, turn & 1

        @pl.when(turn == 0)
        def _():
            for t in range(4):
                for w in range(2):
                    for n, half in pieces:
                        fetch(spots_of(t, w)[n], half).start()

                @pl.when(live_ref[t] > 0)
                def _():
                    for w in range(2):
                        bring(t, w).start()

        @pl.when(step > 0)
        def _():
            for n, half in pieces:
                send(step - 1, which, n, half).wait()

        spots = spots_of(step, which)
        for n, half in pieces:
            fetch(spots[n], half).wait()

        @pl.when(live_ref[step] > 0)
        def _():
            bring(step, which).wait()
            ahead = jnp.where(which == 0, spots[0], spots[1])
            behind = jnp.where(which == 0, spots[1], spots[0])

            def side(spot):
                flat = [d_ref[spot, :, low].reshape(high * 8, LANES) for low in range(wide)]
                return jnp.concatenate(flat, axis=1)

            def keep(n, at, value):
                for low in range(PIECE // LANES):
                    part = value[:, low * LANES : (low + 1) * LANES].astype(BF16)
                    u_ref[which, n, :, at // LANES + low] = part.reshape(high, 8, LANES)

            upper, lower = side(ahead), side(behind)
            for n in range(0, AREA, PIECE):
                keep(1 - which, n, mm(upper, t_ref[step, which, :, pl.ds(n, PIECE)], NN))
                keep(which, n, mm(lower, t_ref[step, which, pl.ds(n, PIECE), :], NT))

        @pl.when(live_ref[step] == 0)
        def _():
            u_ref[which] = jnp.zeros(u_ref.shape[1:], BF16)

        for n, half in pieces:
            send(step, which, n, half).start()

        @pl.when(turn == 7)
        def _():
            for w in range(2):
                for n, half in pieces:
                    send(3, w, n, half).wait()
        return carry

    lax.fori_loop(0, 8, one, 0)


def contract_call(live, tiles, fetched, dens):
    parts, corners, _, _ = fetched.shape
    shape = (dens // 8, AREA // LANES, 2, corners, 4, LANES)
    updates = pl.pallas_call(
        contract_kernel,
        out_shape=pltpu.HBM(shape, BF16),
        in_specs=[
            pl.BlockSpec(memory_space=pltpu.SMEM),
            pl.BlockSpec(memory_space=pl.ANY),
            pl.BlockSpec(memory_space=pl.ANY),
        ],
        out_specs=pl.BlockSpec(memory_space=pl.ANY),
        scratch_shapes=[
            pltpu.VMEM(tiles.shape, BF16),
            pltpu.VMEM((corners, dens // 8, AREA // LANES, 8, LANES), BF16),
            pltpu.VMEM((2, 2, dens // 8, AREA // LANES, 8, LANES), BF16),
            pltpu.SemaphoreType.DMA((4, 2)),
            pltpu.SemaphoreType.DMA((corners, 2)),
            pltpu.SemaphoreType.DMA((2, 2, 2)),
        ],
        compiler_params=pltpu.CompilerParams(vmem_limit_bytes=48 * 1024 * 1024),
        cost_estimate=pl.CostEstimate(flops=6_000_000_000, bytes_accessed=20_000_000, transcendentals=0),
    )(live, tiles, fetched.reshape(shape))
    return updates.reshape(fetched.shape)


def split_kernel(bra_ref, ket_ref, slot_ref, list_ref, count_ref, in_ref, out_ref, live_ref, buf_ref, in_sems, out_sems):
    count, dens, area = in_ref.shape
    each = 2 * area // LANES
    groups = dens // 8
    for g in range(groups):
        for part in range(each):
            rows, low = pl.ds(g * 8 + part % 2 * 4, 4), part // 2
            pltpu.make_async_copy(
                in_ref.at[:, rows, pl.ds(low * LANES, LANES)],
                buf_ref.at[g * each + part, pl.ds(0, count)],
                in_sems.at[g, part],
            ).start()
    slots = [slot_ref[bra_ref[0, n // 2, n % 2]] for n in range(4)]
    slots += [slot_ref[ket_ref[0, n // 2, n % 2]] for n in range(4)]
    live = []
    for task in range(4):
        hit = 0
        for n in range(4):
            hit = hit + jnp.where((list_ref[0, n] == task) & (n < count_ref[0]), 1, 0)
        live.append(hit)
        live_ref[task] = hit
    lane = lax.broadcasted_iota(jnp.int32, (4, LANES), 1)
    head = jnp.zeros((4, LANES), jnp.int32)
    for n, value in enumerate(slots + live):
        head = jnp.where(lane == n, value, head)
    head = head.astype(F32).astype(BF16)
    for part in range(groups * each):
        buf_ref[part, count] = head
    outs = []
    for g in range(groups):
        for part in range(each):
            rows, low = pl.ds(g * 8 + part % 2 * 4, 4), part // 2
            pltpu.make_async_copy(
                in_ref.at[:, rows, pl.ds(low * LANES, LANES)],
                buf_ref.at[g * each + part, pl.ds(0, count)],
                in_sems.at[g, part],
            ).wait()
        at = pl.ds(g * each, each)
        outs.append(pltpu.make_async_copy(buf_ref.at[at], out_ref.at[at], out_sems.at[g]))
        outs[g].start()
    for g in range(groups):
        outs[g].wait()


def split_call(bra, ket, slot, tasks, counts, blocks):
    count, dens, area = blocks.shape
    each = 2 * area // LANES
    shape = (dens // 8 * each, count + 1, 4, LANES)
    smem = pl.BlockSpec(memory_space=pltpu.SMEM)
    hbm = pl.BlockSpec(memory_space=pl.ANY)
    return pl.pallas_call(
        split_kernel,
        out_shape=(pltpu.HBM(shape, BF16), jax.ShapeDtypeStruct((4,), jnp.int32)),
        in_specs=[smem] * 5 + [hbm],
        out_specs=(hbm, smem),
        scratch_shapes=[
            pltpu.VMEM(shape, BF16),
            pltpu.SemaphoreType.DMA((dens // 8, each)),
            pltpu.SemaphoreType.DMA((dens // 8,)),
        ],
        compiler_params=pltpu.CompilerParams(vmem_limit_bytes=60 * 1024 * 1024),
    )(bra, ket, slot, tasks, counts, blocks)


def join_kernel(most_ref, slot_ref, in_ref, more_ref, out_ref, zero_ref, sems):
    count = out_ref.shape[0]
    wide, cap = in_ref.shape[1], in_ref.shape[3]
    zero_ref[...] = jnp.zeros(zero_ref.shape, BF16)

    def fill(block, ref, slot):
        for low in range(wide):
            for half in range(2):
                to = out_ref.at[block, :, pl.ds(half * 4, 4), pl.ds(low * LANES, LANES)]
                pltpu.make_async_copy(ref.at[:, low, half, slot], to, sems.at[block]).start()

    def one(block, carry):
        slot = slot_ref[block]

        @pl.when(slot < 0)
        def _():
            pltpu.make_async_copy(zero_ref, out_ref.at[block], sems.at[block]).start()

        @pl.when((slot >= 0) & (slot < cap))
        def _():
            fill(block, in_ref, slot)

        @pl.when(slot >= cap)
        def _():
            fill(block, more_ref, slot - cap)

        return carry

    lax.fori_loop(0, count, one, 0)

    def done(block, carry):
        pltpu.make_async_copy(zero_ref, out_ref.at[block], sems.at[block]).wait()
        return carry

    lax.fori_loop(0, count, done, 0)


def join_call(most, slots, parts, more, count, dens, area):
    smem = pl.BlockSpec(memory_space=pltpu.SMEM)
    tall, wide = dens // 8, area // LANES

    def view(x):
        return x.reshape(tall, wide, 2, x.shape[1], 4, LANES)

    blocks = pl.pallas_call(
        join_kernel,
        out_shape=pltpu.HBM((count, tall, 8, area), BF16),
        in_specs=[smem, smem, pl.BlockSpec(memory_space=pltpu.VMEM), pl.BlockSpec(memory_space=pl.ANY)],
        out_specs=pl.BlockSpec(memory_space=pl.ANY),
        scratch_shapes=[pltpu.VMEM((tall, 8, area), BF16), pltpu.SemaphoreType.DMA((count,))],
        compiler_params=pltpu.CompilerParams(vmem_limit_bytes=32 * 1024 * 1024),
    )(most, slots, view(parts), view(more))
    return blocks.reshape(count, dens, area)


def gather_kernel(token_ref, in_ref, out_ref, table_ref, after_ref, rows_ref, head_ref, at_ref, spot_ref, sems):
    after_ref[0] = token_ref[0]
    owners, stride = in_ref.shape[0], in_ref.shape[1]
    step = pl.program_id(0)
    near = out_ref.shape[0]

    @pl.when(step == 0)
    def _():
        heads = pltpu.make_async_copy(in_ref.at[:, stride - 1], head_ref, sems.at[0])
        heads.start()
        rest = pltpu.make_async_copy(in_ref, rows_ref, sems.at[1])
        rest.start()
        heads.wait()

        def pull(owner, carry):
            head = head_ref[owner].astype(F32)[0:1]
            table_ref[pl.ds(owner, 1), :] = head.astype(jnp.int32)
            return carry

        lax.fori_loop(0, owners, pull, 0, unroll=8)
        table = table_ref[...]
        lane = lax.broadcasted_iota(jnp.int32, table.shape, 1)
        down = (table >> 3) * 16
        across = table >> 2
        inside = jnp.where(lane < 4, (table & 7) * 4, table & 3)
        at_ref[...] = jnp.where(lane < 4, down, across) * stride + inside
        copy = pltpu.make_async_copy(at_ref, spot_ref, sems.at[2])
        copy.start()
        copy.wait()
        rest.wait()

    flat = rows_ref.reshape(owners * stride, 4, LANES)

    def one(n, carry):
        owner = step * near + n
        downs = [spot_ref[owner, n] for n in range(4)]
        acrosses = [spot_ref[owner, 4 + n] for n in range(4)]
        for corner in range(16):
            out_ref[n, corner] = flat[downs[corner // 4] + acrosses[corner % 4]]
        return carry

    lax.fori_loop(0, near, one, 0, unroll=4)


def gather_call(token, rows):
    smem = pl.BlockSpec(memory_space=pltpu.SMEM)
    owners = rows.shape[0]
    near = owners // 2
    return pl.pallas_call(
        gather_kernel,
        out_shape=(
            pltpu.HBM((owners, 16, 4, LANES), BF16),
            pltpu.HBM((owners, LANES), jnp.int32),
            jax.ShapeDtypeStruct((1,), jnp.int32),
        ),
        grid=(2,),
        in_specs=[smem, pl.BlockSpec(memory_space=pl.ANY)],
        out_specs=(
            pl.BlockSpec((near, 16, 4, LANES), lambda g: (g, 0, 0, 0)),
            pl.BlockSpec((owners, LANES), lambda g: (0, 0)),
            smem,
        ),
        scratch_shapes=[
            pltpu.VMEM(rows.shape, BF16),
            pltpu.VMEM((owners, 4, LANES), BF16),
            pltpu.VMEM((owners, LANES), jnp.int32),
            pltpu.SMEM((owners, LANES), jnp.int32),
            pltpu.SemaphoreType.DMA((3,)),
        ],
        compiler_params=pltpu.CompilerParams(vmem_limit_bytes=60 * 1024 * 1024),
    )(token, rows)


def plan_kernel(table_ref, at_ref, ranks_ref):
    table = table_ref[...]
    owners = table.shape[0]
    size = ranks_ref.shape[0]
    ids = lax.broadcasted_iota(jnp.int32, (owners, size), 1)
    hot = [(table[:, n : n + 1] == ids).astype(F32) for n in range(8)]
    live = [table[:, n : n + 1].astype(F32) for n in range(8, 12)]
    xs, ys = hot[:4], hot[4:]
    both = [ys[0] + ys[1], ys[2] + ys[3]]
    count = 0.0
    for pair in range(2):
        across = live[2 * pair] * both[0] + live[2 * pair + 1] * both[1]
        count = count + mm(xs[2 * pair] + xs[2 * pair + 1], across, ((0,), (0,)))
    used = (count > 0.5).astype(F32)
    a = lax.broadcasted_iota(jnp.int32, (size, size), 0)
    b = lax.broadcasted_iota(jnp.int32, (size, size), 1)
    above = ((a // 8 == b // 8) & (b < a)).astype(F32)
    beside = (a // 4 == b // 4).astype(F32)
    before = ((a // 4 == b // 4) & (a < b)).astype(F32)
    rank = mm(mm(above, used, NN), beside, NN) + mm(used, before, NN)
    ranks_ref[...] = jnp.where(used > 0.5, rank, -1.0).astype(jnp.int32)
    for i in range(4):
        mine = mm(xs[i], rank, NN)
        for j in range(4):
            n = i * 4 + j
            found = jnp.sum(mine * ys[j], axis=1, keepdims=True)
            dev = table[:, i : i + 1] // 8 * 16 + table[:, 4 + j : 5 + j] // 4
            at_ref[:, n : n + 1] = (dev * 32 + found.astype(jnp.int32)) * 4


def plan_call(table, size):
    owners = table.shape[0]
    return pl.pallas_call(
        plan_kernel,
        out_shape=(
            pltpu.HBM((owners, 16), jnp.int32),
            jax.ShapeDtypeStruct((size, size), jnp.int32),
        ),
    )(table)


def scatter_kernel(most_ref, at_ref, in_ref, out_ref, more_ref, sum_ref, spot_ref, sem):
    near, cap = out_ref.shape[0], out_ref.shape[1]
    room = cap + more_ref.shape[1]
    devices = sum_ref.shape[0] // (room * 4)
    crowded = most_ref[0] > cap
    step = pl.program_id(0)

    @pl.when(step == 0)
    def _():
        copy = pltpu.make_async_copy(at_ref, spot_ref, sem)
        copy.start()

        def clear(dev, carry):
            sum_ref[pl.ds(pl.multiple_of(dev * room * 4, 8), cap * 4)] = jnp.zeros((cap * 4, LANES), F32)
            return carry

        lax.fori_loop(0, devices, clear, 0, unroll=4)

        @pl.when(crowded)
        def _():
            def clear_more(dev, carry):
                sum_ref[pl.ds(pl.multiple_of((dev * room + cap) * 4, 8), (room - cap) * 4)] = jnp.zeros(((room - cap) * 4, LANES), F32)
                return carry
            lax.fori_loop(0, devices, clear_more, 0)

        copy.wait()

        def one(owner, carry):
            spots = [pl.ds(pl.multiple_of(spot_ref[owner, n], 4), 4) for n in range(16)]
            sums = [sum_ref[spots[n]] + in_ref[owner, n].astype(F32) for n in range(16)]
            for n in range(16):
                sum_ref[spots[n]] = sums[n]
            return carry

        lax.fori_loop(0, in_ref.shape[0], one, 0, unroll=4)

    def finish(n, carry):
        at = pl.ds(pl.multiple_of((step * near + n) * room * 4, 8), cap * 4)
        out_ref[n] = sum_ref[at].astype(BF16).reshape(cap, 4, LANES)
        return carry

    lax.fori_loop(0, near, finish, 0, unroll=4)

    @pl.when(crowded)
    def _():
        def finish_more(n, carry):
            at = pl.ds(pl.multiple_of(((step * near + n) * room + cap) * 4, 8), (room - cap) * 4)
            more_ref[n] = sum_ref[at].astype(BF16).reshape(room - cap, 4, LANES)
            return carry
        lax.fori_loop(0, near, finish_more, 0)


def scatter_call(most, at, updates, devices, cap, room):
    smem = pl.BlockSpec(memory_space=pltpu.SMEM)
    near = devices // 2
    return pl.pallas_call(
        scatter_kernel,
        out_shape=(
            pltpu.HBM((devices, cap, 4, LANES), BF16),
            pltpu.HBM((devices, room - cap, 4, LANES), BF16),
        ),
        grid=(2,),
        in_specs=[smem, pl.BlockSpec(memory_space=pltpu.HBM), pl.BlockSpec(memory_space=pltpu.VMEM)],
        out_specs=(
            pl.BlockSpec((near, cap, 4, LANES), lambda g: (g, 0, 0, 0)),
            pl.BlockSpec((near, room - cap, 4, LANES), lambda g: (g, 0, 0, 0)),
        ),
        scratch_shapes=[
            pltpu.VMEM((devices * room * 4, LANES), F32),
            pltpu.SMEM(at.shape, jnp.int32),
            pltpu.SemaphoreType.DMA,
        ],
        compiler_params=pltpu.CompilerParams(vmem_limit_bytes=40 * 1024 * 1024),
    )(most, at, updates)


def exchange_all(x):
    return lax.all_to_all(x, AXES, split_axis=0, concat_axis=0, tiled=True)


def shards(density, bra_factor, ket_factor, bra_blocks, ket_blocks, block_slot, task_list, task_count):
    n_col = lax.axis_size("col")
    devices = lax.axis_size("row") * n_col
    blk_row, blk_col, dens, area = density.shape
    local = blk_row * blk_col

    outgoing, live = split_call(
        bra_blocks, ket_blocks, block_slot, task_list, task_count, density.reshape(local, dens, area)
    )
    arrived = exchange_all(outgoing)
    tiles, token = tiles_call(0, 3, live, live, bra_factor[0], ket_factor[0], live)
    picked, table, token = gather_call(token, arrived)
    fetched = exchange_all(picked)

    tiles, _ = tiles_call(3, 1, live, token, bra_factor[0], ket_factor[0], tiles)
    at, ranks = plan_call(table, block_slot.shape[0])
    most = (jnp.max(ranks) + 1).reshape(1)
    corner = (lax.axis_index("row") * blk_row, lax.axis_index("col") * blk_col)
    mine = lax.dynamic_slice(ranks, corner, (blk_row, blk_col)).reshape(local)
    updates = contract_call(live, tiles, fetched, dens)

    returned = exchange_all(updates)
    total, more = scatter_call(most, at, returned, devices, CAP, local)
    parts = exchange_all(total)
    more = lax.cond(most[0] > CAP, exchange_all, lambda x: x, more)
    final = join_call(most, mine, parts, more, local, dens, area)
    return final.reshape(blk_row, blk_col, dens, area)


def solution(mesh):
    in_specs = (
        P("row", "col", None, None),
        P(AXES, None, None, None),
        P(AXES, None, None, None),
        P(AXES, None, None),
        P(AXES, None, None),
        P(),
        P(AXES, None),
        P(AXES),
    )
    out_specs = P("row", "col", None, None)
    return jax.shard_map(shards, mesh=mesh, in_specs=in_specs, out_specs=out_specs, check_vma=False)
```
